32 devices in a mesh: row: 4 (over x, core), col: 8 (over z, y).
Axes of the slice: x: 2, y: 2, z: 4, core: 2. Of those that a mesh axis runs over, the one named last changes fastest.
Arguments:
- amps: bfloat16 [4096, 4096], P(('row', 'col')), may hold values from -6 to 6
- integrals: bfloat16 [4096, 4096], P('row', 'col'), may hold values from -0.125 to 0.125
- amplitude_tile_mask: int32 [32, 32], P('row', 'col'), may hold values from 0 to 1, as said below
- integral_tile_mask: int32 [32, 32], P('row', 'col'), may hold values 0 or 1
Outputs:
- ladder: float32 [4096, 4096], P('row', 'col')
The draws below stay inside these ranges and needn't reach their ends.
Inputs may be any that keep to these rules, and one draw needn't show every extreme that they name: `amplitude_tile_mask`: in every tile row, each aligned group of 4 tile columns holds exactly 2 nonzero tiles.
All inputs are finite; a program needn't handle non-finite values. No bound on the sum of `integral_tile_mask` on one device may be relied on, other than what follows from the above.
Results may differ from the reference program's by a relative error of at most 0.0003.
Values may be sent and summed in bfloat16 or wider, within the bound.
No kernel may reach another device: no remote copies, remote signals or barrier semaphores. Data moves between devices by JAX's collectives and lax.ppermute only.
A program may use at most 128 MiB of HBM per device.

```python
import jax
import jax.numpy as jnp

TILE_EDGE = 128
KT_DEV = 4
MT = 32
KT = 32
NT = 32
M = 4096
K = 4096
N = 4096


def draw_amplitude_tile_mask(key, part):
    groups = KT // KT_DEV
    scores = jax.random.randint(key, (MT, groups, KT_DEV), 0, 1 << 20) * KT_DEV + jnp.arange(KT_DEV, dtype=jnp.int32)
    ranks = jnp.argsort(jnp.argsort(scores, axis=2), axis=2)
    return (ranks < KT_DEV // 2).astype(jnp.int32).reshape(MT, KT)


def place_ends(values, key, least, high):
    place = [jax.random.randint(jax.random.fold_in(key, axis), (), 0, length) for axis, length in enumerate(values.shape)]
    widest = values.shape.index(max(values.shape))
    next_to = place[:widest] + [(place[widest] + 1) % values.shape[widest]] + place[widest + 1:]
    return values.at[tuple(place)].set(least).at[tuple(next_to)].set(high)


def block_scale(own_key, dims, pieces, low, high):
    level, own = 1.0, jax.random.fold_in(own_key, 6)
    for axis_at, parts in pieces:
        draws = jnp.exp(jax.random.uniform(jax.random.fold_in(own, axis_at), (parts,), jnp.float32, low / len(pieces), high / len(pieces)))
        level = level * jnp.repeat(draws, dims[axis_at] // parts).reshape([-1 if axis == axis_at else 1 for axis in range(len(dims))])
    return level


def bell_draw(own_key, extent, width, reach, shards=(), held_as=jnp.bfloat16):
    level = block_scale(own_key, extent, shards, -0.22, 0.18) if shards else 1.0
    values = jax.random.normal(own_key, extent, jnp.float32) * width * level
    return jnp.minimum(jnp.maximum(values, -reach), reach).astype(held_as)


def setup_inputs(seed: int = 0) -> dict:
    arg_keys = jax.random.split(jax.random.key(seed), 5)
    return {
        "amps": bell_draw(arg_keys[0], (M, K), 1.0, 6.0, ((0, 32),)),
        "integrals": bell_draw(arg_keys[1], (K, N), (K // 2) ** -0.5, 0.125, ((0, 4), (1, 8))),
        "amplitude_tile_mask": draw_amplitude_tile_mask(jax.random.fold_in(arg_keys[4], 71), 0),
        "integral_tile_mask": place_ends((jax.random.randint(arg_keys[3], (KT, NT), 0, 2) < 1).astype(jnp.int32), jax.random.fold_in(arg_keys[3], 1), 0, 1),
    }


def reference(amps, integrals, amplitude_tile_mask, integral_tile_mask):
    outer_tile_count, inner_tile_count = amplitude_tile_mask.shape
    ntiles = integral_tile_mask.shape[1]
    sparse_amplitude_tiles = (amps.reshape(outer_tile_count, TILE_EDGE, inner_tile_count, TILE_EDGE) * amplitude_tile_mask[:, None, :, None].astype(amps.dtype)).reshape(amps.shape)
    sparse_ints = (integrals.reshape(inner_tile_count, TILE_EDGE, ntiles, TILE_EDGE) * integral_tile_mask[:, None, :, None].astype(integrals.dtype)).reshape(integrals.shape)
    return jnp.dot(sparse_amplitude_tiles, sparse_ints, preferred_element_type=jnp.float32)
```

```python
import functools

import jax
import jax.numpy as jnp
from jax import lax
from jax.experimental import pallas as pl
from jax.experimental.pallas import tpu as pltpu
from jax.sharding import PartitionSpec as P

TILE = 128
GROUP = 4
KEEP = 2
VMEM_LIMIT = 40 * 1024 * 1024

_smem = pl.BlockSpec(memory_space=pltpu.SMEM)
_vmem = pl.BlockSpec(memory_space=pltpu.VMEM)
_any = pl.BlockSpec(memory_space=pl.ANY)


def ring_chip(pos, n):
    return jnp.where(pos < n // 2, 2 * pos, 2 * (n - 1 - pos) + 1)


def ring_pos(c, n):
    return jnp.where(c % 2 == 0, c // 2, n - 1 - c // 2)


def picks(mask_ref, row, first):
    m0, m1 = mask_ref[row, first], mask_ref[row, first + 1]
    m2, m3 = mask_ref[row, first + 2], mask_ref[row, first + 3]
    lo = jnp.where(m0 != 0, 0, jnp.where(m1 != 0, 1, 2))
    hi = jnp.where(m3 != 0, 3, jnp.where(m2 != 0, 2, 1))
    return lo, hi


def mask_ints_kernel(mask_ref, x_ref, o_ref):
    kt, nt = mask_ref.shape
    for q in range(kt):
        for n in range(nt):
            at = (pl.ds(q * TILE, TILE), pl.ds(n * TILE, TILE))
            x = x_ref[at]
            o_ref[at] = jnp.where(mask_ref[q, n] != 0, x, jnp.zeros_like(x))


def compress_kernel(n_row, kt_local, mask_ref, a_ref, *refs):
    outs, sem = refs[:-1], refs[-1]
    rows = a_ref.shape[0]
    r, c = lax.axis_index("row"), lax.axis_index("col")
    row = c * rows // TILE
    per_out = n_row // len(outs)
    copies = []
    for j in range(n_row):
        block = jnp.bitwise_xor(r, j)
        out, j_in = outs[j // per_out], j % per_out
        for g in range(kt_local // GROUP):
            first = block * kt_local + g * GROUP
            for s, p in enumerate(picks(mask_ref, row, first)):
                slot = (j_in * (kt_local // GROUP) + g) * KEEP + s
                src = pl.multiple_of((first + p) * TILE, TILE)
                copies.append(
                    pltpu.make_async_copy(
                        a_ref.at[:, pl.ds(src, TILE)],
                        out.at[:, pl.ds(slot * TILE, TILE)],
                        sem.at[len(copies)],
                    )
                )
    for copy in copies:
        copy.start()
    for copy in copies:
        copy.wait()


def ladder_kernel(n_row, n_col, shifts, mask_ref, *refs):
    n_units = 2 * len(shifts)
    units, ints = refs[:n_units], refs[n_units : n_units + n_row]
    o_ref, acc, sem = refs[-3:]
    rows = units[0].shape[0]
    kt_local = ints[0].shape[0] // TILE
    per_unit = n_row // 2
    r, c = lax.axis_index("row"), lax.axis_index("col")
    pos = ring_pos(c, n_col)
    copies = []
    for i, shift in enumerate(shifts):
        src = ring_chip(lax.rem(pos + (n_col - shift), n_col), n_col)
        row = src * rows // TILE
        total = jnp.zeros(acc.shape[1:], jnp.float32)
        for j in range(n_row):
            block = jnp.bitwise_xor(r, j)
            unit, j_in = units[2 * i + j // per_unit], j % per_unit
            for g in range(kt_local // GROUP):
                lo, hi = picks(mask_ref, row, block * kt_local + g * GROUP)
                rhs = jnp.concatenate(
                    [ints[j][pl.ds(pl.multiple_of((g * GROUP + p) * TILE, TILE), TILE), :] for p in (lo, hi)], axis=0
                )
                at = (j_in * (kt_local // GROUP) + g) * KEEP * TILE
                total += jnp.dot(unit[:, at : at + KEEP * TILE], rhs, preferred_element_type=jnp.float32)
        acc[i] = total
        copy = pltpu.make_async_copy(acc.at[i], o_ref.at[pl.ds(pl.multiple_of(src * rows, rows), rows), :], sem.at[i])
        copy.start()
        copies.append(copy)
    for copy in copies:
        copy.wait()


def ladder_rows(n_row, n_col, shifts, mask, units, ints, out_shape, out):
    rows, cols = units[0][0].shape[0], out_shape.shape[1]
    flat = [u for pair in units for u in pair]
    args = [mask, *flat, *ints]
    specs = [_smem] + [_vmem] * (len(flat) + len(ints))
    alias = {}
    if out is not None:
        alias = {len(args): 0}
        args.append(out)
        specs.append(_any)
    return pl.pallas_call(
        functools.partial(ladder_kernel, n_row, n_col, shifts),
        out_shape=out_shape,
        in_specs=specs,
        out_specs=_any,
        scratch_shapes=[pltpu.VMEM((len(shifts), rows, cols), jnp.float32), pltpu.SemaphoreType.DMA((len(shifts),))],
        input_output_aliases=alias,
        compiler_params=pltpu.CompilerParams(vmem_limit_bytes=VMEM_LIMIT),
    )(*args)


def on_device(n_row, n_col, amps, integrals, amplitude_tile_mask, integral_tile_mask):
    rows, depth = amps.shape
    tile_rows, kblock = amplitude_tile_mask.shape
    kt_local = integrals.shape[0] // TILE
    r, c = lax.axis_index("row"), lax.axis_index("col")

    sparse_ints = pl.pallas_call(
        mask_ints_kernel,
        out_shape=jax.ShapeDtypeStruct(integrals.shape, integrals.dtype),
        in_specs=[_smem, _vmem],
        out_specs=_vmem,
        compiler_params=pltpu.CompilerParams(vmem_limit_bytes=VMEM_LIMIT),
    )(integral_tile_mask, integrals)
    ints = [None] * n_row
    for j in range(0, n_row, 2):
        ints[j] = sparse_ints if j == 0 else lax.ppermute(sparse_ints, "row", [(i, i ^ j) for i in range(n_row)])
    for j in range(0, n_row, 2):
        ints[j + 1] = lax.ppermute(ints[j], "row", [(i, i ^ 1) for i in range(n_row)])

    mine = lax.broadcasted_iota(jnp.int32, (tile_rows, n_col * kblock), 1) // kblock == c
    mask = lax.psum(jnp.where(mine, jnp.tile(amplitude_tile_mask, (1, n_col)), 0), "col")

    half = (rows, depth * KEEP // GROUP // 2)
    own = pl.pallas_call(
        functools.partial(compress_kernel, n_row, kt_local),
        out_shape=[jax.ShapeDtypeStruct(half, amps.dtype)] * 2,
        in_specs=[_smem, _any],
        out_specs=[_vmem] * 2,
        scratch_shapes=[pltpu.SemaphoreType.DMA((depth // TILE * KEEP // GROUP,))],
        compiler_params=pltpu.CompilerParams(vmem_limit_bytes=VMEM_LIMIT),
    )(mask, amps)

    order = [2 * p if p < n_col // 2 else 2 * (n_col - 1 - p) + 1 for p in range(n_col)]
    up = [(order[p], order[(p + 1) % n_col]) for p in range(n_col)]
    down = [(d, s) for s, d in up]
    out_shape = jax.ShapeDtypeStruct((rows * n_col, integrals.shape[1]), jnp.float32)

    fwd, bwd = own, own
    held = {0: own}
    for k in range(1, n_col // 2):
        nf, nb = [], []
        for h in range(2):
            nf.append(lax.ppermute(fwd[h], "col", up))
            nb.append(lax.ppermute(bwd[h], "col", down))
        fwd, bwd = nf, nb
        held[k], held[n_col - k] = fwd, bwd
    held[n_col // 2] = [lax.ppermute(fwd[0], "col", up), lax.ppermute(bwd[1], "col", down)]

    out = None
    groups = [(0, 1, n_col - 1)] + [(k, n_col - k) for k in range(2, n_col // 2)] + [(n_col // 2,)]
    for shifts in groups:
        out = ladder_rows(n_row, n_col, shifts, mask, [held[s] for s in shifts], ints, out_shape, out)
    return out


def solution(mesh):
    placed = (P(("row", "col"), None), P("row", "col"), P("row", "col"), P("row", "col"))
    return jax.shard_map(
        functools.partial(on_device, mesh.shape["row"], mesh.shape["col"]),
        mesh=mesh,
        in_specs=placed,
        out_specs=P("row", "col"),
        check_vma=False,
    )
```

```python
import functools

import jax
import jax.numpy as jnp
from jax import lax
from jax.experimental import pallas as pl
from jax.experimental.pallas import tpu as pltpu
from jax.sharding import PartitionSpec as P

TILE = 128
GROUP = 4
KEEP = 2
VMEM_LIMIT = 40 * 1024 * 1024

_smem = pl.BlockSpec(memory_space=pltpu.SMEM)
_vmem = pl.BlockSpec(memory_space=pltpu.VMEM)
_hbm = pl.BlockSpec(memory_space=pltpu.HBM)
_any = pl.BlockSpec(memory_space=pl.ANY)
_params = pltpu.CompilerParams(vmem_limit_bytes=VMEM_LIMIT)


def ring_chip(pos, n):
    return jnp.where(pos < n // 2, 2 * pos, 2 * (n - 1 - pos) + 1)


def ring_pos(c, n):
    return jnp.where(c % 2 == 0, c // 2, n - 1 - c // 2)


def picks(mask_ref, row, first):
    m0, m1 = mask_ref[row, first], mask_ref[row, first + 1]
    m2, m3 = mask_ref[row, first + 2], mask_ref[row, first + 3]
    lo = jnp.where(m0 != 0, 0, jnp.where(m1 != 0, 1, 2))
    hi = jnp.where(m3 != 0, 3, jnp.where(m2 != 0, 2, 1))
    return lo, hi


def mask_ints_kernel(mask_ref, x_ref, *refs):
    outs, buf, sem = refs[:-2], refs[-2], refs[-1]
    nt, kt = mask_ref.shape
    copies = []
    for g in range(len(outs)):
        at = pl.ds(g * GROUP * TILE, GROUP * TILE)
        copies.append(pltpu.make_async_copy(x_ref.at[at, :], buf.at[g], sem.at[g]))
        copies[-1].start()
    for g, out in enumerate(outs):
        copies[g].wait()
        for q in range(GROUP):
            for t in range(nt):
                at = (pl.ds(q * TILE, TILE), pl.ds(t * TILE, TILE))
                x = buf[g, at[0], at[1]]
                out[at] = jnp.where(mask_ref[t, g * GROUP + q] != 0, x, jnp.zeros_like(x))


def compress_kernel(n_row, kt_local, mask_ref, a_ref, *refs):
    outs, sem = refs[:-1], refs[-1]
    rows = a_ref.shape[0]
    r, c = lax.axis_index("row"), lax.axis_index("col")
    row = c * rows // TILE
    per_out = n_row // len(outs)
    copies = []
    for j in range(n_row):
        block = jnp.bitwise_xor(r, j)
        out, j_in = outs[j // per_out], j % per_out
        for g in range(kt_local // GROUP):
            first = block * kt_local + g * GROUP
            for s, p in enumerate(picks(mask_ref, row, first)):
                slot = (j_in * (kt_local // GROUP) + g) * KEEP + s
                src = pl.multiple_of((first + p) * TILE, TILE)
                copies.append(
                    pltpu.make_async_copy(
                        a_ref.at[:, pl.ds(src, TILE)],
                        out.at[:, pl.ds(slot * TILE, TILE)],
                        sem.at[len(copies)],
                    )
                )
    for copy in copies:
        copy.start()
    for copy in copies:
        copy.wait()


def ladder_kernel(n_row, n_col, kt_local, shifts, mask_ref, *refs):
    n_units = 2 * len(shifts)
    units, ints = refs[:n_units], refs[n_units:]
    o_ref, acc, sem = refs[-3:]
    rows = units[0].shape[0]
    per_unit = n_row // 2
    r, c = lax.axis_index("row"), lax.axis_index("col")
    pos = ring_pos(c, n_col)
    copies = []
    for i, shift in enumerate(shifts):
        src = ring_chip(lax.rem(pos + (n_col - shift), n_col), n_col)
        row = src * rows // TILE
        total = jnp.zeros(acc.shape[1:], jnp.float32)
        for j in range(n_row):
            block = jnp.bitwise_xor(r, j)
            unit, j_in = units[2 * i + j // per_unit], j % per_unit
            for g in range(kt_local // GROUP):
                lo, hi = picks(mask_ref, row, block * kt_local + g * GROUP)
                held = ints[j * (kt_local // GROUP) + g]
                rhs = jnp.concatenate([held[pl.ds(pl.multiple_of(p * TILE, TILE), TILE), :] for p in (lo, hi)], axis=0)
                at = (j_in * (kt_local // GROUP) + g) * KEEP * TILE
                total += jnp.dot(unit[:, at : at + KEEP * TILE], rhs, preferred_element_type=jnp.float32)
        acc[i] = total
        copy = pltpu.make_async_copy(acc.at[i], o_ref.at[pl.ds(pl.multiple_of(src * rows, rows), rows), :], sem.at[i])
        copy.start()
        copies.append(copy)
    for copy in copies:
        copy.wait()


def ladder_rows(n_row, n_col, kt_local, shifts, mask, units, ints, out_shape, out):
    rows, cols = units[0][0].shape[0], out_shape.shape[1]
    flat = [u for pair in units for u in pair]
    args = [mask, *flat, *ints]
    specs = [_smem] + [_vmem] * (len(flat) + len(ints))
    alias = {}
    if out is not None:
        alias = {len(args): 0}
        args.append(out)
        specs.append(_any)
    return pl.pallas_call(
        functools.partial(ladder_kernel, n_row, n_col, kt_local, shifts),
        out_shape=out_shape,
        in_specs=specs,
        out_specs=_any,
        scratch_shapes=[pltpu.VMEM((len(shifts), rows, cols), jnp.float32), pltpu.SemaphoreType.DMA((len(shifts),))],
        input_output_aliases=alias,
        compiler_params=_params,
    )(*args)


def on_device(n_row, n_col, amps, integrals, amplitude_tile_mask, integral_tile_mask):
    rows, depth = amps.shape
    tile_rows, kblock = amplitude_tile_mask.shape
    kt_local = integrals.shape[0] // TILE
    n_groups = kt_local // GROUP
    c = lax.axis_index("col")
    piece = jax.ShapeDtypeStruct((GROUP * TILE, integrals.shape[1]), integrals.dtype)

    def masked_ints(x):
        return pl.pallas_call(
            mask_ints_kernel,
            out_shape=[piece] * n_groups,
            in_specs=[_smem, _hbm],
            out_specs=[_vmem] * n_groups,
            scratch_shapes=[pltpu.VMEM((n_groups, *piece.shape), piece.dtype), pltpu.SemaphoreType.DMA((n_groups,))],
            compiler_params=_params,
        )(integral_tile_mask.T, x)

    mine = lax.broadcasted_iota(jnp.int32, (tile_rows, n_col * kblock), 1) // kblock == c
    mask = lax.psum(jnp.where(mine, jnp.tile(amplitude_tile_mask, (1, n_col)), 0), "col")

    half = (rows, depth * KEEP // GROUP // 2)
    own = pl.pallas_call(
        functools.partial(compress_kernel, n_row, kt_local),
        out_shape=[jax.ShapeDtypeStruct(half, amps.dtype)] * 2,
        in_specs=[_smem, _hbm],
        out_specs=[_vmem] * 2,
        scratch_shapes=[pltpu.SemaphoreType.DMA((depth // TILE * KEEP // GROUP,))],
        compiler_params=_params,
    )(mask, amps)

    order = [2 * p if p < n_col // 2 else 2 * (n_col - 1 - p) + 1 for p in range(n_col)]
    up = [(order[p], order[(p + 1) % n_col]) for p in range(n_col)]
    down = [(d, s) for s, d in up]
    out_shape = jax.ShapeDtypeStruct((rows * n_col, integrals.shape[1]), jnp.float32)

    last = n_col // 2
    held = {k: [None, None] for k in range(n_col)}
    held[0] = list(own)
    turns = [(k, t) for k in range(1, last + 1) for t in range(2 if k < last else 1)]
    for k, t in turns:
        b = (n_col - k) % n_col
        held[k][t] = lax.ppermute(held[k - 1][t], "col", up)
        held[b][1 - t] = lax.ppermute(held[(b + 1) % n_col][1 - t], "col", down)

    def after(turn, values):
        if turn is None:
            return values
        k, t = turns[turn]
        b = (n_col - k) % n_col
        *values, held[k][t], held[b][1 - t] = lax.optimization_barrier((*values, held[k][t], held[b][1 - t]))
        return values

    def swap(x, j):
        return lax.ppermute(x, "row", [(i, i ^ j) for i in range(n_row)])

    x = integrals
    if True:
        own = list(own)
        x, own[0], own[1] = lax.optimization_barrier((x, own[0], own[1]))
        held[0] = [own[0], own[1]]
    pieces = {0: list(masked_ints(x))}
    for j in range(2, n_row, 2):
        pieces[j] = list((swap(p, j) for p in pieces[0]))
    for j in range(0, n_row, 2):
        pieces[j + 1] = [None] * n_groups
        for g in range(n_groups):
            (pieces[j][g],) = after({(0, 0): 1, (0, 1): 2, (2, 0): 3, (2, 1): 4}[(min(j, 2), g)], (pieces[j][g],))
            pieces[j + 1][g] = swap(pieces[j][g], 1)
    ints = [p for j in range(n_row) for p in pieces[j]]

    out = None
    for shifts in [(0, 1, n_col - 1)] + [(k, n_col - k) for k in range(2, last)] + [(last,)]:
        out = ladder_rows(n_row, n_col, kt_local, shifts, mask, [held[s] for s in shifts], ints, out_shape, out)
    return out


def solution(mesh):
    placed = (P(("row", "col"), None), P("row", "col"), P("row", "col"), P("row", "col"))
    return jax.shard_map(
        functools.partial(on_device, mesh.shape["row"], mesh.shape["col"]),
        mesh=mesh,
        in_specs=placed,
        out_specs=P("row", "col"),
        check_vma=False,
    )
```

```python
import functools

import jax
import jax.numpy as jnp
from jax import lax
from jax.experimental import pallas as pl
from jax.experimental.pallas import tpu as pltpu
from jax.sharding import PartitionSpec as P

TILE = 128
GROUP = 4
KEEP = 2
VMEM_LIMIT = 40 * 1024 * 1024

_smem = pl.BlockSpec(memory_space=pltpu.SMEM)
_vmem = pl.BlockSpec(memory_space=pltpu.VMEM)
_hbm = pl.BlockSpec(memory_space=pltpu.HBM)
_any = pl.BlockSpec(memory_space=pl.ANY)
_params = pltpu.CompilerParams(vmem_limit_bytes=VMEM_LIMIT)


def ring_chip(pos, n):
    return jnp.where(pos < n // 2, 2 * pos, 2 * (n - 1 - pos) + 1)


def ring_pos(c, n):
    return jnp.where(c % 2 == 0, c // 2, n - 1 - c // 2)


def picks(mask_ref, row, first):
    m0, m1 = mask_ref[row, first], mask_ref[row, first + 1]
    m2, m3 = mask_ref[row, first + 2], mask_ref[row, first + 3]
    lo = jnp.where(m0 != 0, 0, jnp.where(m1 != 0, 1, 2))
    hi = jnp.where(m3 != 0, 3, jnp.where(m2 != 0, 2, 1))
    return lo, hi


def mask_ints_kernel(mask_ref, x_ref, *refs):
    outs, buf, sem = refs[:-2], refs[-2], refs[-1]
    nt, kt = mask_ref.shape
    copies = []
    for g in range(len(outs)):
        at = pl.ds(g * GROUP * TILE, GROUP * TILE)
        copies.append(pltpu.make_async_copy(x_ref.at[at, :], buf.at[g], sem.at[g]))
        copies[-1].start()
    for g, out in enumerate(outs):
        copies[g].wait()
        for q in range(GROUP):
            for t in range(nt):
                at = (pl.ds(q * TILE, TILE), pl.ds(t * TILE, TILE))
                x = buf[g, at[0], at[1]]
                out[at] = jnp.where(mask_ref[t, g * GROUP + q] != 0, x, jnp.zeros_like(x))


def compress_kernel(n_row, kt_local, mask_ref, a_ref, *refs):
    outs, sem = refs[:-1], refs[-1]
    rows = a_ref.shape[0]
    r, c = lax.axis_index("row"), lax.axis_index("col")
    row = c * rows // TILE
    per_out = n_row // len(outs)
    copies = []
    for j in range(n_row):
        block = jnp.bitwise_xor(r, j)
        out, j_in = outs[j // per_out], j % per_out
        for g in range(kt_local // GROUP):
            first = block * kt_local + g * GROUP
            for s, p in enumerate(picks(mask_ref, row, first)):
                slot = (j_in * (kt_local // GROUP) + g) * KEEP + s
                src = pl.multiple_of((first + p) * TILE, TILE)
                copies.append(
                    pltpu.make_async_copy(
                        a_ref.at[:, pl.ds(src, TILE)],
                        out.at[:, pl.ds(slot * TILE, TILE)],
                        sem.at[len(copies)],
                    )
                )
    for copy in copies:
        copy.start()
    for copy in copies:
        copy.wait()


def ladder_kernel(n_row, n_col, kt_local, shifts, ahead, mask_ref, *refs):
    n_units = 2 * len(shifts)
    n_ints = n_row * (kt_local // GROUP)
    units, ints = refs[:n_units], refs[n_units : n_units + n_ints]
    acc, sem = refs[-2:]
    o_ref, next_ref = (refs[-3], None) if ahead is None else (refs[-4], refs[-3])
    rows = units[0].shape[0]
    per_unit = n_row // 2
    r, c = lax.axis_index("row"), lax.axis_index("col")

    def source(shift):
        return ring_chip(lax.rem(ring_pos(c, n_col) + (n_col - shift), n_col), n_col)

    def tiles(row, j, g):
        first = (jnp.bitwise_xor(r, j) * (kt_local // GROUP) + g) * GROUP
        held = ints[j * (kt_local // GROUP) + g]
        return [held[pl.ds(pl.multiple_of(p * TILE, TILE), TILE), :] for p in picks(mask_ref, row, first)]

    copies = []
    for i, shift in enumerate(shifts):
        src = source(shift)
        total = jnp.zeros(acc.shape[1:], jnp.float32)
        for j in range(n_row):
            unit, j_in = units[2 * i + j // per_unit], j % per_unit
            for g in range(kt_local // GROUP):
                rhs = jnp.concatenate(tiles(src * rows // TILE, j, g), axis=0)
                at = (j_in * (kt_local // GROUP) + g) * KEEP * TILE
                total += jnp.dot(unit[:, at : at + KEEP * TILE], rhs, preferred_element_type=jnp.float32)
        acc[i] = total
        copy = pltpu.make_async_copy(acc.at[i], o_ref.at[pl.ds(pl.multiple_of(src * rows, rows), rows), :], sem.at[i])
        copy.start()
        copies.append(copy)
    if ahead is not None:
        row = source(ahead) * rows // TILE
        for j in range(n_row):
            for g in range(kt_local // GROUP):
                for s, tile in enumerate(tiles(row, j, g)):
                    at = ((j * (kt_local // GROUP) + g) * KEEP + s) * TILE
                    next_ref[at : at + TILE, :] = tile
    for copy in copies:
        copy.wait()


def last_kernel(n_col, shift, *refs):
    lo, hi, ints, _, o_ref, acc, sem = refs
    rows, depth = lo.shape
    pos = ring_pos(lax.axis_index("col"), n_col)
    src = ring_chip(lax.rem(pos + (n_col - shift), n_col), n_col)
    total = jnp.dot(lo[...], ints[:depth, :], preferred_element_type=jnp.float32)
    acc[...] = total + jnp.dot(hi[...], ints[depth:, :], preferred_element_type=jnp.float32)
    copy = pltpu.make_async_copy(acc, o_ref.at[pl.ds(pl.multiple_of(src * rows, rows), rows), :], sem)
    copy.start()
    copy.wait()


def ladder_rows(n_row, n_col, kt_local, shifts, ahead, mask, units, ints, out_shape, out):
    rows, cols = units[0][0].shape[0], out_shape.shape[1]
    flat = [u for pair in units for u in pair]
    args = [mask, *flat, *ints]
    specs = [_smem] + [_vmem] * (len(flat) + len(ints))
    alias = {}
    if out is not None:
        alias = {len(args): 0}
        args.append(out)
        specs.append(_any)
    shapes, places = [out_shape], [_any]
    if ahead is not None:
        shapes.append(jax.ShapeDtypeStruct((2 * flat[0].shape[1], cols), ints[0].dtype))
        places.append(_vmem)
    return pl.pallas_call(
        functools.partial(ladder_kernel, n_row, n_col, kt_local, shifts, ahead),
        out_shape=shapes,
        in_specs=specs,
        out_specs=places,
        scratch_shapes=[pltpu.VMEM((len(shifts), rows, cols), jnp.float32), pltpu.SemaphoreType.DMA((len(shifts),))],
        input_output_aliases=alias,
        compiler_params=_params,
    )(*args)


def on_device(n_row, n_col, amps, integrals, amplitude_tile_mask, integral_tile_mask):
    rows, depth = amps.shape
    tile_rows, kblock = amplitude_tile_mask.shape
    kt_local = integrals.shape[0] // TILE
    n_groups = kt_local // GROUP
    c = lax.axis_index("col")
    piece = jax.ShapeDtypeStruct((GROUP * TILE, integrals.shape[1]), integrals.dtype)

    def masked_ints(x):
        return pl.pallas_call(
            mask_ints_kernel,
            out_shape=[piece] * n_groups,
            in_specs=[_smem, _hbm],
            out_specs=[_vmem] * n_groups,
            scratch_shapes=[pltpu.VMEM((n_groups, *piece.shape), piece.dtype), pltpu.SemaphoreType.DMA((n_groups,))],
            compiler_params=_params,
        )(integral_tile_mask.T, pltpu.with_memory_space_constraint(x, pltpu.HBM))

    mine = lax.broadcasted_iota(jnp.int32, (tile_rows, n_col * kblock), 1) // kblock == c
    mask = lax.psum(jnp.where(mine, jnp.tile(amplitude_tile_mask, (1, n_col)), 0), "col")

    half = (rows, depth * KEEP // GROUP // 2)
    own = pl.pallas_call(
        functools.partial(compress_kernel, n_row, kt_local),
        out_shape=[jax.ShapeDtypeStruct(half, amps.dtype)] * 2,
        in_specs=[_smem, _hbm],
        out_specs=[_vmem] * 2,
        scratch_shapes=[pltpu.SemaphoreType.DMA((depth // TILE * KEEP // GROUP,))],
        compiler_params=_params,
    )(mask, pltpu.with_memory_space_constraint(amps, pltpu.HBM))

    order = [2 * p if p < n_col // 2 else 2 * (n_col - 1 - p) + 1 for p in range(n_col)]
    up = [(order[p], order[(p + 1) % n_col]) for p in range(n_col)]
    down = [(d, s) for s, d in up]
    out_shape = jax.ShapeDtypeStruct((rows * n_col, integrals.shape[1]), jnp.float32)

    last = n_col // 2
    held = {k: [None, None] for k in range(n_col)}
    held[0] = list(own)
    turns = [(k, t) for k in range(1, last + 1) for t in range(2 if k < last else 1)]
    for k, t in turns:
        b = (n_col - k) % n_col
        held[k][t] = lax.ppermute(held[k - 1][t], "col", up)
        held[b][1 - t] = lax.ppermute(held[(b + 1) % n_col][1 - t], "col", down)

    def after(turn, values, way):
        if turn is None:
            return values
        k, t = turns[turn]
        b = (n_col - k) % n_col
        if way != "d":
            *values, held[k][t] = lax.optimization_barrier((*values, held[k][t]))
        if way != "u":
            *values, held[b][1 - t] = lax.optimization_barrier((*values, held[b][1 - t]))
        return values

    def swap(x, j):
        return lax.ppermute(x, "row", [(i, i ^ j) for i in range(n_row)])

    x = integrals
    if True:
        own = list(own)
        x, own[0], own[1] = lax.optimization_barrier((x, own[0], own[1]))
        held[0] = [own[0], own[1]]
    pieces = {0: list(masked_ints(x))}
    for j in range(2, n_row, 2):
        late = [pieces[0][0], *after(1, pieces[0][1:], 'b')]
        pieces[j] = [swap(p, j) for p in late]
    for j in range(0, n_row, 2):
        pieces[j + 1] = [None] * n_groups
        for g in range(n_groups):
            (pieces[j][g],) = after((0, 4, 4, 5)[min(j, 2) + g], (pieces[j][g],), 'bbub'[min(j, 2) + g])
            pieces[j + 1][g] = swap(pieces[j][g], 1)
    ints = [p for j in range(n_row) for p in pieces[j]]

    out = None
    groups = [(0, 1, n_col - 1, 2, n_col - 2)] + [(k, n_col - k) for k in range(3, last)]
    for shifts in groups:
        ahead = last if shifts == groups[-1] else None
        out, *tiles = ladder_rows(n_row, n_col, kt_local, shifts, ahead, mask, [held[s] for s in shifts], ints, out_shape, out)
    return pl.pallas_call(
        functools.partial(last_kernel, n_col, last),
        out_shape=out_shape,
        in_specs=[_vmem] * 3 + [_any],
        out_specs=_any,
        scratch_shapes=[pltpu.VMEM((rows, integrals.shape[1]), jnp.float32), pltpu.SemaphoreType.DMA],
        input_output_aliases={3: 0},
        compiler_params=_params,
    )(*held[last], *tiles, out)


def solution(mesh):
    placed = (P(("row", "col"), None), P("row", "col"), P("row", "col"), P("row", "col"))
    return jax.shard_map(
        functools.partial(on_device, mesh.shape["row"], mesh.shape["col"]),
        mesh=mesh,
        in_specs=placed,
        out_specs=P("row", "col"),
        check_vma=False,
    )
```

```python
import functools

import jax
import jax.numpy as jnp
from jax import lax
from jax.experimental import pallas as pl
from jax.experimental.pallas import tpu as pltpu
from jax.sharding import PartitionSpec as P

TILE = 128
GROUP = 4
KEEP = 2
VMEM_LIMIT = 40 * 1024 * 1024

_smem = pl.BlockSpec(memory_space=pltpu.SMEM)
_vmem = pl.BlockSpec(memory_space=pltpu.VMEM)
_hbm = pl.BlockSpec(memory_space=pltpu.HBM)
_any = pl.BlockSpec(memory_space=pl.ANY)
_params = pltpu.CompilerParams(vmem_limit_bytes=VMEM_LIMIT)


def ring_chip(pos, n):
    return jnp.where(pos < n // 2, 2 * pos, 2 * (n - 1 - pos) + 1)


def ring_pos(c, n):
    return jnp.where(c % 2 == 0, c // 2, n - 1 - c // 2)


def picks(mask_ref, tile_rows, row, group):
    m0, m1, m2, m3 = (mask_ref[i, group * tile_rows + row] for i in range(GROUP))
    lo = jnp.where(m0 != 0, 0, jnp.where(m1 != 0, 1, 2))
    hi = jnp.where(m3 != 0, 3, jnp.where(m2 != 0, 2, 1))
    return lo, hi


def mask_ints_kernel(mask_ref, x_ref, *refs):
    outs, buf, sem = refs[:-2], refs[-2], refs[-1]
    nt, kt = mask_ref.shape
    copies = []
    for g in range(len(outs)):
        at = pl.ds(g * GROUP * TILE, GROUP * TILE)
        copies.append(pltpu.make_async_copy(x_ref.at[at, :], buf.at[g], sem.at[g]))
        copies[-1].start()
    for g, out in enumerate(outs):
        copies[g].wait()
        for q in range(GROUP):
            for t in range(nt):
                at = (pl.ds(q * TILE, TILE), pl.ds(t * TILE, TILE))
                x = buf[g, at[0], at[1]]
                out[at] = jnp.where(mask_ref[t, g * GROUP + q] != 0, x, jnp.zeros_like(x))


def stage_kernel(mask_ref, a_ref, o_ref, held_ref, m_ref, sem):
    half = a_ref.shape[0] // 2
    copies = [
        pltpu.make_async_copy(a_ref.at[pl.ds(i * half, half), :], held_ref.at[pl.ds(i * half, half), :], sem.at[i]) for i in range(2)
    ]
    copies.insert(0, pltpu.make_async_copy(mask_ref, m_ref, sem.at[2]))
    for copy in copies:
        copy.start()
    tile_rows, wide = m_ref.shape[1], o_ref.shape[1]
    row = lax.broadcasted_iota(jnp.int32, (tile_rows, wide), 0)
    at = lax.broadcasted_iota(jnp.int32, (tile_rows, wide), 1)
    spread = (at == lax.axis_index("col") * tile_rows + row).astype(jnp.float32).astype(jnp.bfloat16)
    copies.pop(0).wait()
    piece = m_ref[...].astype(jnp.float32).astype(jnp.bfloat16)
    o_ref[...] = jnp.dot(piece, spread, preferred_element_type=jnp.float32).astype(jnp.int32)
    for copy in copies:
        copy.wait()


def compress_kernel(n_row, n_col, tile_rows, mask_ref, a_ref, *outs):
    rows, depth = a_ref.shape
    wide = GROUP * TILE
    n_groups = depth // wide // n_row
    r, c = lax.axis_index("row"), lax.axis_index("col")
    mask = mask_ref[...].astype(jnp.float32)
    at = lax.broadcasted_iota(jnp.int32, mask.shape, 1)
    per_out = n_row // len(outs)
    for j in range(n_row):
        out, j_in = outs[j // per_out], j % per_out
        for g in range(n_groups):
            group = jnp.bitwise_xor(r, j) * n_groups + g
            m = jnp.sum(jnp.where(at == group * tile_rows + c * rows // TILE, mask, 0.0), axis=1, keepdims=True)
            m0, m1, m2, m3 = (m[i : i + 1, :] for i in range(GROUP))
            low = (m0, (1 - m0) * m1, (1 - m0) * (1 - m1))
            high = (m3, (1 - m3) * m2, (1 - m3) * (1 - m2))
            x = [a_ref[:, pl.ds(pl.multiple_of(group * wide + i * TILE, TILE), TILE)] for i in range(GROUP)]
            slot = (j_in * n_groups + g) * KEEP
            for s, (weights, order) in enumerate(((low, (0, 1, 2)), (high, (3, 2, 1)))):
                parts = [x[i] * jnp.broadcast_to(w, x[i].shape).astype(x[i].dtype) for w, i in zip(weights, order)]
                out[:, (slot + s) * TILE : (slot + s + 1) * TILE] = parts[0] + parts[1] + parts[2]


def ladder_kernel(n_row, n_col, kt_local, shifts, ahead, mask_ref, *refs):
    n_units = 2 * len(shifts)
    n_ints = n_row * (kt_local // GROUP)
    units, ints = refs[:n_units], refs[n_units : n_units + n_ints]
    acc, sem = refs[-2:]
    o_ref, next_ref = (refs[-3], None) if ahead is None else (refs[-4], refs[-3])
    rows = units[0].shape[0]
    per_unit = n_row // 2
    tile_rows = n_col * rows // TILE
    r, c = lax.axis_index("row"), lax.axis_index("col")

    def source(shift):
        return ring_chip(lax.rem(ring_pos(c, n_col) + (n_col - shift), n_col), n_col)

    def tiles(row, j, g):
        group = jnp.bitwise_xor(r, j) * (kt_local // GROUP) + g
        held = ints[j * (kt_local // GROUP) + g]
        return [held[pl.ds(pl.multiple_of(p * TILE, TILE), TILE), :] for p in picks(mask_ref, tile_rows, row, group)]

    copies = []
    for i, shift in enumerate(shifts):
        src = source(shift)
        total = jnp.zeros(acc.shape[1:], jnp.float32)
        for j in range(n_row):
            unit, j_in = units[2 * i + j // per_unit], j % per_unit
            for g in range(kt_local // GROUP):
                rhs = jnp.concatenate(tiles(src * rows // TILE, j, g), axis=0)
                at = (j_in * (kt_local // GROUP) + g) * KEEP * TILE
                total += jnp.dot(unit[:, at : at + KEEP * TILE], rhs, preferred_element_type=jnp.float32)
        acc[i] = total
        copy = pltpu.make_async_copy(acc.at[i], o_ref.at[pl.ds(pl.multiple_of(src * rows, rows), rows), :], sem.at[i])
        copy.start()
        copies.append(copy)
    if ahead is not None:
        row = source(ahead) * rows // TILE
        for j in range(n_row):
            for g in range(kt_local // GROUP):
                for s, tile in enumerate(tiles(row, j, g)):
                    at = ((j * (kt_local // GROUP) + g) * KEEP + s) * TILE
                    next_ref[at : at + TILE, :] = tile
    for copy in copies:
        copy.wait()


def last_kernel(n_col, shift, *refs):
    lo, hi, ints, _, o_ref, acc, sem = refs
    rows, depth = lo.shape
    pos = ring_pos(lax.axis_index("col"), n_col)
    src = ring_chip(lax.rem(pos + (n_col - shift), n_col), n_col)
    total = jnp.dot(lo[...], ints[:depth, :], preferred_element_type=jnp.float32)
    acc[...] = total + jnp.dot(hi[...], ints[depth:, :], preferred_element_type=jnp.float32)
    copy = pltpu.make_async_copy(acc, o_ref.at[pl.ds(pl.multiple_of(src * rows, rows), rows), :], sem)
    copy.start()
    copy.wait()


def ladder_rows(n_row, n_col, kt_local, shifts, ahead, mask, units, ints, out_shape, out):
    rows, cols = units[0][0].shape[0], out_shape.shape[1]
    flat = [u for pair in units for u in pair]
    args = [mask, *flat, *ints]
    specs = [_smem] + [_vmem] * (len(flat) + len(ints))
    alias = {}
    if out is not None:
        alias = {len(args): 0}
        args.append(out)
        specs.append(_any)
    shapes, places = [out_shape], [_any]
    if ahead is not None:
        shapes.append(jax.ShapeDtypeStruct((2 * flat[0].shape[1], cols), ints[0].dtype))
        places.append(_vmem)
    return pl.pallas_call(
        functools.partial(ladder_kernel, n_row, n_col, kt_local, shifts, ahead),
        out_shape=shapes,
        in_specs=specs,
        out_specs=places,
        scratch_shapes=[pltpu.VMEM((len(shifts), rows, cols), jnp.float32), pltpu.SemaphoreType.DMA((len(shifts),))],
        input_output_aliases=alias,
        compiler_params=_params,
    )(*args)


def on_device(n_row, n_col, amps, integrals, amplitude_tile_mask, integral_tile_mask):
    rows, depth = amps.shape
    tile_rows, kblock = amplitude_tile_mask.shape
    kt_local = integrals.shape[0] // TILE
    n_groups = kt_local // GROUP
    piece = jax.ShapeDtypeStruct((GROUP * TILE, integrals.shape[1]), integrals.dtype)

    def masked_ints(x):
        return pl.pallas_call(
            mask_ints_kernel,
            out_shape=[piece] * n_groups,
            in_specs=[_smem, _hbm],
            out_specs=[_vmem] * n_groups,
            scratch_shapes=[pltpu.VMEM((n_groups, *piece.shape), piece.dtype), pltpu.SemaphoreType.DMA((n_groups,))],
            compiler_params=_params,
        )(integral_tile_mask.T, pltpu.with_memory_space_constraint(x, pltpu.HBM))

    placed, amps = pl.pallas_call(
        stage_kernel,
        out_shape=[
            jax.ShapeDtypeStruct((kblock, n_col * tile_rows), jnp.int32),
            jax.ShapeDtypeStruct(amps.shape, amps.dtype),
        ],
        in_specs=[_hbm, _hbm],
        out_specs=[_vmem] * 2,
        scratch_shapes=[pltpu.VMEM((kblock, tile_rows), jnp.int32), pltpu.SemaphoreType.DMA((3,))],
        compiler_params=_params,
    )(pltpu.with_memory_space_constraint(amplitude_tile_mask.T, pltpu.HBM), pltpu.with_memory_space_constraint(amps, pltpu.HBM))
    mask = lax.psum(placed, "col")

    half = (rows, depth * KEEP // GROUP // 2)
    own = pl.pallas_call(
        functools.partial(compress_kernel, n_row, n_col, tile_rows),
        out_shape=[jax.ShapeDtypeStruct(half, amps.dtype)] * 2,
        in_specs=[_vmem, _vmem],
        out_specs=[_vmem] * 2,
        compiler_params=_params,
    )(mask, amps)

    order = [2 * p if p < n_col // 2 else 2 * (n_col - 1 - p) + 1 for p in range(n_col)]
    up = [(order[p], order[(p + 1) % n_col]) for p in range(n_col)]
    down = [(d, s) for s, d in up]
    out_shape = jax.ShapeDtypeStruct((rows * n_col, integrals.shape[1]), jnp.float32)

    last = n_col // 2
    held = {k: [None, None] for k in range(n_col)}
    held[0] = list(own)
    turns = [(k, t) for k in range(1, last + 1) for t in range(2 if k < last else 1)]
    for k, t in turns:
        b = (n_col - k) % n_col
        held[k][t] = lax.ppermute(held[k - 1][t], "col", up)
        held[b][1 - t] = lax.ppermute(held[(b + 1) % n_col][1 - t], "col", down)

    def after(turn, values, way):
        if turn is None:
            return values
        k, t = turns[turn]
        b = (n_col - k) % n_col
        if way != "d":
            *values, held[k][t] = lax.optimization_barrier((*values, held[k][t]))
        if way != "u":
            *values, held[b][1 - t] = lax.optimization_barrier((*values, held[b][1 - t]))
        return values

    def swap(x, j):
        return lax.ppermute(x, "row", [(i, i ^ j) for i in range(n_row)])

    late, *held[0] = lax.optimization_barrier((integrals, *held[0]))
    pieces = {0: list(masked_ints(late))}
    for j in range(2, n_row, 2):
        late = [pieces[0][0], *after(1, pieces[0][1:], 'b')]
        pieces[j] = [swap(p, j) for p in late]
    for j in range(0, n_row, 2):
        pieces[j + 1] = [None] * n_groups
        for g in range(n_groups):
            (pieces[j][g],) = after((0, 4, 4, 5)[min(j, 2) + g], (pieces[j][g],), 'bbub'[min(j, 2) + g])
            pieces[j + 1][g] = swap(pieces[j][g], 1)
    ints = [p for j in range(n_row) for p in pieces[j]]

    out = None
    groups = [(0, 1, n_col - 1, 2, n_col - 2)] + [(k, n_col - k) for k in range(3, last)]
    for shifts in groups:
        ahead = last if shifts == groups[-1] else None
        out, *tiles = ladder_rows(n_row, n_col, kt_local, shifts, ahead, mask, [held[s] for s in shifts], ints, out_shape, out)
    return pl.pallas_call(
        functools.partial(last_kernel, n_col, last),
        out_shape=out_shape,
        in_specs=[_vmem] * 3 + [_any],
        out_specs=_any,
        scratch_shapes=[pltpu.VMEM((rows, integrals.shape[1]), jnp.float32), pltpu.SemaphoreType.DMA],
        input_output_aliases={3: 0},
        compiler_params=_params,
    )(*held[last], *tiles, out)


def solution(mesh):
    placed = (P(("row", "col"), None), P("row", "col"), P("row", "col"), P("row", "col"))
    return jax.shard_map(
        functools.partial(on_device, mesh.shape["row"], mesh.shape["col"]),
        mesh=mesh,
        in_specs=placed,
        out_specs=P("row", "col"),
        check_vma=False,
    )
```

```python
import functools

import jax
import jax.numpy as jnp
from jax import lax
from jax.experimental import pallas as pl
from jax.experimental.pallas import tpu as pltpu
from jax.sharding import PartitionSpec as P

TILE = 128
GROUP = 4
KEEP = 2
VMEM_LIMIT = 40 * 1024 * 1024

_smem = pl.BlockSpec(memory_space=pltpu.SMEM)
_vmem = pl.BlockSpec(memory_space=pltpu.VMEM)
_hbm = pl.BlockSpec(memory_space=pltpu.HBM)
_any = pl.BlockSpec(memory_space=pl.ANY)
_params = pltpu.CompilerParams(vmem_limit_bytes=VMEM_LIMIT)


def ring_chip(pos, n):
    return jnp.where(pos < n // 2, 2 * pos, 2 * (n - 1 - pos) + 1)


def ring_pos(c, n):
    return jnp.where(c % 2 == 0, c // 2, n - 1 - c // 2)


def picks(mask_ref, tile_rows, row, group):
    m0, m1, m2, m3 = (mask_ref[i, group * tile_rows + row] for i in range(GROUP))
    lo = jnp.where(m0 != 0, 0, jnp.where(m1 != 0, 1, 2))
    hi = jnp.where(m3 != 0, 3, jnp.where(m2 != 0, 2, 1))
    return lo, hi


def stage_kernel(mask_ref, a_ref, int_mask_ref, x_ref, o_ref, held_ref, *refs):
    pieces, (m_ref, sem), inner, (held_mask, mask_sem) = refs[:-6], refs[-6:-4], refs[-4:-2], refs[-2:]
    load = pltpu.make_async_copy(int_mask_ref, held_mask, mask_sem)
    load.start()
    half = a_ref.shape[0] // 2
    copies = [
        pltpu.make_async_copy(a_ref.at[pl.ds(i * half, half), :], held_ref.at[pl.ds(i * half, half), :], sem.at[i]) for i in range(2)
    ]
    loads = []
    for g in range(len(pieces)):
        loads.append(pltpu.make_async_copy(x_ref.at[pl.ds(g * GROUP * TILE, GROUP * TILE), :], inner[0].at[g], inner[1].at[g]))
    copies.insert(0, pltpu.make_async_copy(mask_ref, m_ref, sem.at[2]))
    for copy in copies[:1] + loads + copies[1:]:
        copy.start()
    tile_rows, wide = m_ref.shape[1], o_ref.shape[1]
    row = lax.broadcasted_iota(jnp.int32, (tile_rows, wide), 0)
    at = lax.broadcasted_iota(jnp.int32, (tile_rows, wide), 1)
    spread = (at == lax.axis_index("col") * tile_rows + row).astype(jnp.float32).astype(jnp.bfloat16)
    copies.pop(0).wait()
    piece = m_ref[...].astype(jnp.float32).astype(jnp.bfloat16)
    o_ref[...] = jnp.dot(piece, spread, preferred_element_type=jnp.float32).astype(jnp.int32)
    load.wait()
    for g, out in enumerate(pieces):
        loads[g].wait()
        for q in range(GROUP):
            for t in range(held_mask.shape[0]):
                at = (pl.ds(q * TILE, TILE), pl.ds(t * TILE, TILE))
                x = inner[0][g, at[0], at[1]]
                out[at] = jnp.where(held_mask[t, g * GROUP + q] != 0, x, jnp.zeros_like(x))
    for copy in copies:
        copy.wait()


def compress_kernel(n_row, n_col, tile_rows, mask_ref, a_ref, *outs):
    rows, depth = a_ref.shape
    wide = GROUP * TILE
    n_groups = depth // wide // n_row
    r, c = lax.axis_index("row"), lax.axis_index("col")
    mask = mask_ref[...].astype(jnp.float32)
    at = lax.broadcasted_iota(jnp.int32, mask.shape, 1)
    per_out = n_row // len(outs)
    for j in range(n_row):
        out, j_in = outs[j // per_out], j % per_out
        for g in range(n_groups):
            group = jnp.bitwise_xor(r, j) * n_groups + g
            m = jnp.sum(jnp.where(at == group * tile_rows + c * rows // TILE, mask, 0.0), axis=1, keepdims=True)
            m0, m1, m2, m3 = (m[i : i + 1, :] for i in range(GROUP))
            low = (m0, (1 - m0) * m1, (1 - m0) * (1 - m1))
            high = (m3, (1 - m3) * m2, (1 - m3) * (1 - m2))
            x = [a_ref[:, pl.ds(pl.multiple_of(group * wide + i * TILE, TILE), TILE)] for i in range(GROUP)]
            slot = (j_in * n_groups + g) * KEEP
            for s, (weights, order) in enumerate(((low, (0, 1, 2)), (high, (3, 2, 1)))):
                parts = [x[i] * jnp.broadcast_to(w, x[i].shape).astype(x[i].dtype) for w, i in zip(weights, order)]
                out[:, (slot + s) * TILE : (slot + s + 1) * TILE] = parts[0] + parts[1] + parts[2]


def ladder_kernel(n_row, n_col, kt_local, shifts, ahead, mask_ref, *refs):
    n_units = 2 * len(shifts)
    n_ints = n_row * (kt_local // GROUP)
    units, ints = refs[:n_units], refs[n_units : n_units + n_ints]
    acc, sem = refs[-2:]
    o_ref, next_ref = (refs[-3], None) if ahead is None else (refs[-4], refs[-3])
    rows = units[0].shape[0]
    per_unit = n_row // 2
    tile_rows = n_col * rows // TILE
    r, c = lax.axis_index("row"), lax.axis_index("col")

    def source(shift):
        return ring_chip(lax.rem(ring_pos(c, n_col) + (n_col - shift), n_col), n_col)

    def tiles(row, j, g):
        group = jnp.bitwise_xor(r, j) * (kt_local // GROUP) + g
        held = ints[j * (kt_local // GROUP) + g]
        return [held[pl.ds(pl.multiple_of(p * TILE, TILE), TILE), :] for p in picks(mask_ref, tile_rows, row, group)]

    copies = []
    for i, shift in enumerate(shifts):
        src = source(shift)
        total = jnp.zeros(acc.shape[1:], jnp.float32)
        for j in range(n_row):
            unit, j_in = units[2 * i + j // per_unit], j % per_unit
            for g in range(kt_local // GROUP):
                rhs = jnp.concatenate(tiles(src * rows // TILE, j, g), axis=0)
                at = (j_in * (kt_local // GROUP) + g) * KEEP * TILE
                total += jnp.dot(unit[:, at : at + KEEP * TILE], rhs, preferred_element_type=jnp.float32)
        acc[i] = total
        copy = pltpu.make_async_copy(acc.at[i], o_ref.at[pl.ds(pl.multiple_of(src * rows, rows), rows), :], sem.at[i])
        copy.start()
        copies.append(copy)
    if ahead is not None:
        row = source(ahead) * rows // TILE
        for j in range(n_row):
            for g in range(kt_local // GROUP):
                for s, tile in enumerate(tiles(row, j, g)):
                    at = ((j * (kt_local // GROUP) + g) * KEEP + s) * TILE
                    next_ref[at : at + TILE, :] = tile
    for copy in copies:
        copy.wait()


def last_kernel(n_col, shift, *refs):
    lo, hi, ints, _, o_ref, acc, sem = refs
    rows, depth = lo.shape
    pos = ring_pos(lax.axis_index("col"), n_col)
    src = ring_chip(lax.rem(pos + (n_col - shift), n_col), n_col)
    total = jnp.dot(lo[...], ints[:depth, :], preferred_element_type=jnp.float32)
    acc[...] = total + jnp.dot(hi[...], ints[depth:, :], preferred_element_type=jnp.float32)
    copy = pltpu.make_async_copy(acc, o_ref.at[pl.ds(pl.multiple_of(src * rows, rows), rows), :], sem)
    copy.start()
    copy.wait()


def ladder_rows(n_row, n_col, kt_local, shifts, ahead, mask, units, ints, out_shape, out):
    rows, cols = units[0][0].shape[0], out_shape.shape[1]
    flat = [u for pair in units for u in pair]
    args = [mask, *flat, *ints]
    specs = [_smem] + [_vmem] * (len(flat) + len(ints))
    alias = {}
    if out is not None:
        alias = {len(args): 0}
        args.append(out)
        specs.append(_any)
    shapes, places = [out_shape], [_any]
    if ahead is not None:
        shapes.append(jax.ShapeDtypeStruct((2 * flat[0].shape[1], cols), ints[0].dtype))
        places.append(_vmem)
    return pl.pallas_call(
        functools.partial(ladder_kernel, n_row, n_col, kt_local, shifts, ahead),
        out_shape=shapes,
        in_specs=specs,
        out_specs=places,
        scratch_shapes=[pltpu.VMEM((len(shifts), rows, cols), jnp.float32), pltpu.SemaphoreType.DMA((len(shifts),))],
        input_output_aliases=alias,
        compiler_params=_params,
    )(*args)


def on_device(n_row, n_col, amps, integrals, amplitude_tile_mask, integral_tile_mask):
    rows, depth = amps.shape
    tile_rows, kblock = amplitude_tile_mask.shape
    kt_local = integrals.shape[0] // TILE
    n_groups = kt_local // GROUP
    piece = jax.ShapeDtypeStruct((GROUP * TILE, integrals.shape[1]), integrals.dtype)

    placed, amps, *masked = pl.pallas_call(
        stage_kernel,
        out_shape=[
            jax.ShapeDtypeStruct((kblock, n_col * tile_rows), jnp.int32),
            jax.ShapeDtypeStruct(amps.shape, amps.dtype),
            *[piece] * n_groups,
        ],
        in_specs=[_hbm] * 4,
        out_specs=[_vmem] * (2 + n_groups),
        scratch_shapes=[
            pltpu.VMEM((kblock, tile_rows), jnp.int32),
            pltpu.SemaphoreType.DMA((3,)),
            pltpu.VMEM((n_groups, *piece.shape), piece.dtype),
            pltpu.SemaphoreType.DMA((n_groups,)),
            pltpu.SMEM(integral_tile_mask.shape[::-1], jnp.int32),
            pltpu.SemaphoreType.DMA,
        ],
        compiler_params=_params,
    )(
        pltpu.with_memory_space_constraint(amplitude_tile_mask.T, pltpu.HBM),
        pltpu.with_memory_space_constraint(amps, pltpu.HBM),
        pltpu.with_memory_space_constraint(integral_tile_mask.T, pltpu.HBM),
        pltpu.with_memory_space_constraint(integrals, pltpu.HBM),
    )
    def swap(x, j):
        return lax.ppermute(x, "row", [(i, i ^ j) for i in range(n_row)])

    sibling = [swap(p, 1) for p in masked]
    mask = lax.psum(placed, "col")
    amps, *sibling = lax.optimization_barrier((amps, *sibling))

    half = (rows, depth * KEEP // GROUP // 2)
    own = pl.pallas_call(
        functools.partial(compress_kernel, n_row, n_col, tile_rows),
        out_shape=[jax.ShapeDtypeStruct(half, amps.dtype)] * 2,
        in_specs=[_vmem, _vmem],
        out_specs=[_vmem] * 2,
        compiler_params=_params,
    )(mask, amps)

    order = [2 * p if p < n_col // 2 else 2 * (n_col - 1 - p) + 1 for p in range(n_col)]
    up = [(order[p], order[(p + 1) % n_col]) for p in range(n_col)]
    down = [(d, s) for s, d in up]
    out_shape = jax.ShapeDtypeStruct((rows * n_col, integrals.shape[1]), jnp.float32)

    last = n_col // 2
    held = {k: [None, None] for k in range(n_col)}
    held[0] = list(own)
    turns = [(k, t) for k in range(1, last + 1) for t in range(2 if k < last else 1)]
    for k, t in turns:
        b = (n_col - k) % n_col
        held[k][t] = lax.ppermute(held[k - 1][t], "col", up)
        held[b][1 - t] = lax.ppermute(held[(b + 1) % n_col][1 - t], "col", down)

    def after(turn, values, way):
        if turn is None:
            return values
        k, t = turns[turn]
        b = (n_col - k) % n_col
        if way != "d":
            *values, held[k][t] = lax.optimization_barrier((*values, held[k][t]))
        if way != "u":
            *values, held[b][1 - t] = lax.optimization_barrier((*values, held[b][1 - t]))
        return values

    masked[0], masked[1], *held[0] = lax.optimization_barrier((masked[0], masked[1], *held[0]))
    pieces = {0: masked, 1: sibling}
    for j in range(2, n_row, 2):
        pieces[j] = []
        for p, turn in zip(masked, (0, 1)):
            (p,) = after(turn, (p,), "b")
            pieces[j].append(swap(p, j))
        pieces[j + 1] = []
        for g, turn in enumerate((4, 5)):
            (pieces[j][g],) = after(turn, (pieces[j][g],), "b")
            pieces[j + 1].append(swap(pieces[j][g], 1))
    ints = [p for j in range(n_row) for p in pieces[j]]

    out = None
    groups = [(0, 1, n_col - 1, 2, n_col - 2)] + [(k, n_col - k) for k in range(3, last)]
    for shifts in groups:
        ahead = last if shifts == groups[-1] else None
        out, *tiles = ladder_rows(n_row, n_col, kt_local, shifts, ahead, mask, [held[s] for s in shifts], ints, out_shape, out)
    return pl.pallas_call(
        functools.partial(last_kernel, n_col, last),
        out_shape=out_shape,
        in_specs=[_vmem] * 3 + [_any],
        out_specs=_any,
        scratch_shapes=[pltpu.VMEM((rows, integrals.shape[1]), jnp.float32), pltpu.SemaphoreType.DMA],
        input_output_aliases={3: 0},
        compiler_params=_params,
    )(*held[last], *tiles, out)


def solution(mesh):
    placed = (P(("row", "col"), None), P("row", "col"), P("row", "col"), P("row", "col"))
    return jax.shard_map(
        functools.partial(on_device, mesh.shape["row"], mesh.shape["col"]),
        mesh=mesh,
        in_specs=placed,
        out_specs=P("row", "col"),
        check_vma=False,
    )
```

```python
import functools

import jax
import jax.numpy as jnp
from jax import lax
from jax.experimental import pallas as pl
from jax.experimental.pallas import tpu as pltpu
from jax.sharding import PartitionSpec as P

TILE = 128
GROUP = 4
KEEP = 2
VMEM_LIMIT = 40 * 1024 * 1024

_smem = pl.BlockSpec(memory_space=pltpu.SMEM)
_vmem = pl.BlockSpec(memory_space=pltpu.VMEM)
_hbm = pl.BlockSpec(memory_space=pltpu.HBM)
_any = pl.BlockSpec(memory_space=pl.ANY)
_params = pltpu.CompilerParams(vmem_limit_bytes=VMEM_LIMIT)


def ring_chip(pos, n):
    return jnp.where(pos < n // 2, 2 * pos, 2 * (n - 1 - pos) + 1)


def ring_pos(c, n):
    return jnp.where(c % 2 == 0, c // 2, n - 1 - c // 2)


def picks(mask_ref, tile_rows, row, group):
    m0, m1, m2, m3 = (mask_ref[i, group * tile_rows + row] for i in range(GROUP))
    lo = jnp.where(m0 != 0, 0, jnp.where(m1 != 0, 1, 2))
    hi = jnp.where(m3 != 0, 3, jnp.where(m2 != 0, 2, 1))
    return lo, hi


def stage_kernel(mask_ref, a_ref, int_mask_ref, x_ref, o_ref, held_ref, *refs):
    pieces, (m_ref, sem), inner, (held_mask, mask_sem) = refs[:-6], refs[-6:-4], refs[-4:-2], refs[-2:]
    load = pltpu.make_async_copy(int_mask_ref, held_mask, mask_sem)
    load.start()
    half = a_ref.shape[0] // 2
    copies = [
        pltpu.make_async_copy(a_ref.at[pl.ds(i * half, half), :], held_ref.at[pl.ds(i * half, half), :], sem.at[i]) for i in range(2)
    ]
    loads = []
    for g in range(len(pieces)):
        loads.append(pltpu.make_async_copy(x_ref.at[pl.ds(g * GROUP * TILE, GROUP * TILE), :], inner[0].at[g], inner[1].at[g]))
    copies.insert(0, pltpu.make_async_copy(mask_ref, m_ref, sem.at[2]))
    for copy in copies[:1] + loads + copies[1:]:
        copy.start()
    tile_rows, wide = m_ref.shape[1], o_ref.shape[1]
    row = lax.broadcasted_iota(jnp.int32, (tile_rows, wide), 0)
    at = lax.broadcasted_iota(jnp.int32, (tile_rows, wide), 1)
    spread = (at == lax.axis_index("col") * tile_rows + row).astype(jnp.float32).astype(jnp.bfloat16)
    copies.pop(0).wait()
    piece = m_ref[...].astype(jnp.float32).astype(jnp.bfloat16)
    o_ref[...] = jnp.dot(piece, spread, preferred_element_type=jnp.float32).astype(jnp.int32)
    load.wait()
    for g, out in enumerate(pieces):
        loads[g].wait()
        for q in range(GROUP):
            for t in range(held_mask.shape[0]):
                at = (pl.ds(q * TILE, TILE), pl.ds(t * TILE, TILE))
                x = inner[0][g, at[0], at[1]]
                out[at] = jnp.where(held_mask[t, g * GROUP + q] != 0, x, jnp.zeros_like(x))
    for copy in copies:
        copy.wait()


def compress_kernel(n_row, n_col, tile_rows, mask_ref, a_ref, *outs):
    rows, depth = a_ref.shape
    wide = GROUP * TILE
    n_groups = depth // wide // n_row
    r, c = lax.axis_index("row"), lax.axis_index("col")
    mask = mask_ref[...].astype(jnp.float32)
    at = lax.broadcasted_iota(jnp.int32, mask.shape, 1)
    per_out = n_row // len(outs)
    for j in range(n_row):
        out, j_in = outs[j // per_out], j % per_out
        for g in range(n_groups):
            group = jnp.bitwise_xor(r, j) * n_groups + g
            m = jnp.sum(jnp.where(at == group * tile_rows + c * rows // TILE, mask, 0.0), axis=1, keepdims=True)
            m0, m1, m2, m3 = (m[i : i + 1, :] for i in range(GROUP))
            low = (m0, (1 - m0) * m1, (1 - m0) * (1 - m1))
            high = (m3, (1 - m3) * m2, (1 - m3) * (1 - m2))
            x = [a_ref[:, pl.ds(pl.multiple_of(group * wide + i * TILE, TILE), TILE)] for i in range(GROUP)]
            slot = (j_in * n_groups + g) * KEEP
            for s, (weights, order) in enumerate(((low, (0, 1, 2)), (high, (3, 2, 1)))):
                parts = [x[i] * jnp.broadcast_to(w, x[i].shape).astype(x[i].dtype) for w, i in zip(weights, order)]
                out[:, (slot + s) * TILE : (slot + s + 1) * TILE] = parts[0] + parts[1] + parts[2]


def ladder_kernel(n_row, n_col, kt_local, shifts, ahead, mask_ref, *refs):
    n_units = 2 * len(shifts)
    n_ints = n_row * (kt_local // GROUP)
    units, ints = refs[:n_units], refs[n_units : n_units + n_ints]
    acc, sem = refs[-2:]
    o_ref, next_ref = (refs[-3], None) if ahead is None else (refs[-4], refs[-3])
    rows = units[0].shape[0]
    per_unit = n_row // 2
    tile_rows = n_col * rows // TILE
    r, c = lax.axis_index("row"), lax.axis_index("col")

    def source(shift):
        return ring_chip(lax.rem(ring_pos(c, n_col) + (n_col - shift), n_col), n_col)

    def tiles(row, j, g):
        group = jnp.bitwise_xor(r, j) * (kt_local // GROUP) + g
        held = ints[j * (kt_local // GROUP) + g]
        return [held[pl.ds(pl.multiple_of(p * TILE, TILE), TILE), :] for p in picks(mask_ref, tile_rows, row, group)]

    copies = []
    for i, shift in enumerate(shifts):
        src = source(shift)
        total = jnp.zeros(acc.shape[1:], jnp.float32)
        for j in range(n_row):
            unit, j_in = units[2 * i + j // per_unit], j % per_unit
            for g in range(kt_local // GROUP):
                rhs = jnp.concatenate(tiles(src * rows // TILE, j, g), axis=0)
                at = (j_in * (kt_local // GROUP) + g) * KEEP * TILE
                total += jnp.dot(unit[:, at : at + KEEP * TILE], rhs, preferred_element_type=jnp.float32)
        acc[i] = total
        copy = pltpu.make_async_copy(acc.at[i], o_ref.at[pl.ds(pl.multiple_of(src * rows, rows), rows), :], sem.at[i])
        copy.start()
        copies.append(copy)
    if ahead is not None:
        row = source(ahead) * rows // TILE
        for j in range(n_row):
            for g in range(kt_local // GROUP):
                for s, tile in enumerate(tiles(row, j, g)):
                    at = ((j * (kt_local // GROUP) + g) * KEEP + s) * TILE
                    next_ref[at : at + TILE, :] = tile
    for copy in copies:
        copy.wait()


def last_kernel(n_col, shift, *refs):
    lo, hi, ints, _, o_ref, acc, sem = refs
    rows, depth = lo.shape
    pos = ring_pos(lax.axis_index("col"), n_col)
    src = ring_chip(lax.rem(pos + (n_col - shift), n_col), n_col)
    total = jnp.dot(lo[...], ints[:depth, :], preferred_element_type=jnp.float32)
    acc[...] = total + jnp.dot(hi[...], ints[depth:, :], preferred_element_type=jnp.float32)
    copy = pltpu.make_async_copy(acc, o_ref.at[pl.ds(pl.multiple_of(src * rows, rows), rows), :], sem)
    copy.start()
    copy.wait()


def ladder_rows(n_row, n_col, kt_local, shifts, ahead, mask, units, ints, out_shape, out):
    rows, cols = units[0][0].shape[0], out_shape.shape[1]
    flat = [u for pair in units for u in pair]
    args = [mask, *flat, *ints]
    specs = [_smem] + [_vmem] * (len(flat) + len(ints))
    alias = {}
    if out is not None:
        alias = {len(args): 0}
        args.append(out)
        specs.append(_any)
    shapes, places = [out_shape], [_any]
    if ahead is not None:
        shapes.append(jax.ShapeDtypeStruct((2 * flat[0].shape[1], cols), ints[0].dtype))
        places.append(_vmem)
    return pl.pallas_call(
        functools.partial(ladder_kernel, n_row, n_col, kt_local, shifts, ahead),
        out_shape=shapes,
        in_specs=specs,
        out_specs=places,
        scratch_shapes=[pltpu.VMEM((len(shifts), rows, cols), jnp.float32), pltpu.SemaphoreType.DMA((len(shifts),))],
        input_output_aliases=alias,
        compiler_params=_params,
    )(*args)


def on_device(n_row, n_col, amps, integrals, amplitude_tile_mask, integral_tile_mask):
    rows, depth = amps.shape
    tile_rows, kblock = amplitude_tile_mask.shape
    kt_local = integrals.shape[0] // TILE
    n_groups = kt_local // GROUP
    piece = jax.ShapeDtypeStruct((GROUP * TILE, integrals.shape[1]), integrals.dtype)

    placed, amps, *masked = pl.pallas_call(
        stage_kernel,
        out_shape=[
            jax.ShapeDtypeStruct((kblock, n_col * tile_rows), jnp.int32),
            jax.ShapeDtypeStruct(amps.shape, amps.dtype),
            *[piece] * n_groups,
        ],
        in_specs=[_hbm] * 4,
        out_specs=[_vmem] * (2 + n_groups),
        scratch_shapes=[
            pltpu.VMEM((kblock, tile_rows), jnp.int32),
            pltpu.SemaphoreType.DMA((3,)),
            pltpu.VMEM((n_groups, *piece.shape), piece.dtype),
            pltpu.SemaphoreType.DMA((n_groups,)),
            pltpu.SMEM(integral_tile_mask.shape[::-1], jnp.int32),
            pltpu.SemaphoreType.DMA,
        ],
        compiler_params=_params,
    )(
        pltpu.with_memory_space_constraint(amplitude_tile_mask.T, pltpu.HBM),
        pltpu.with_memory_space_constraint(amps, pltpu.HBM),
        pltpu.with_memory_space_constraint(integral_tile_mask.T, pltpu.HBM),
        pltpu.with_memory_space_constraint(integrals, pltpu.HBM),
    )
    def swap(x, j):
        return lax.ppermute(x, "row", [(i, i ^ j) for i in range(n_row)])

    sibling = [swap(p, 1) for p in masked]
    mask = lax.psum(placed, "col")
    amps, *sibling = lax.optimization_barrier((amps, *sibling))

    half = (rows, depth * KEEP // GROUP // 2)
    own = pl.pallas_call(
        functools.partial(compress_kernel, n_row, n_col, tile_rows),
        out_shape=[jax.ShapeDtypeStruct(half, amps.dtype)] * 2,
        in_specs=[_vmem, _vmem],
        out_specs=[_vmem] * 2,
        compiler_params=_params,
    )(mask, amps)

    order = [2 * p if p < n_col // 2 else 2 * (n_col - 1 - p) + 1 for p in range(n_col)]
    up = [(order[p], order[(p + 1) % n_col]) for p in range(n_col)]
    down = [(d, s) for s, d in up]
    out_shape = jax.ShapeDtypeStruct((rows * n_col, integrals.shape[1]), jnp.float32)

    last = n_col // 2
    held = {k: [None, None] for k in range(n_col)}
    held[0] = list(own)
    turns = [(k, t) for k in range(1, last + 1) for t in range(2 if k < last else 1)]
    for k, t in turns:
        b = (n_col - k) % n_col
        held[k][t] = lax.ppermute(held[k - 1][t], "col", up)
        held[b][1 - t] = lax.ppermute(held[(b + 1) % n_col][1 - t], "col", down)

    def after(turn, values, way):
        if turn is None:
            return values
        k, t = turns[turn]
        b = (n_col - k) % n_col
        if way != "d":
            *values, held[k][t] = lax.optimization_barrier((*values, held[k][t]))
        if way != "u":
            *values, held[b][1 - t] = lax.optimization_barrier((*values, held[b][1 - t]))
        return values

    masked[0], masked[1], *held[0] = lax.optimization_barrier((masked[0], masked[1], *held[0]))
    pieces = {0: masked, 1: sibling}
    for j in range(2, n_row, 2):
        pieces[j] = []
        for p, turn in zip(masked, (None, 0)):
            (p,) = after(turn, (p,), "b")
            pieces[j].append(swap(p, j))
        pieces[j + 1] = []
        for g, turn in enumerate((4, 5)):
            (pieces[j][g],) = after(turn, (pieces[j][g],), "b")
            pieces[j + 1].append(swap(pieces[j][g], 1))
    ints = [p for j in range(n_row) for p in pieces[j]]

    out = None
    groups = [(0, 1, n_col - 1, 2, n_col - 2)] + [(k, n_col - k) for k in range(3, last)]
    for shifts in groups:
        ahead = last if shifts == groups[-1] else None
        out, *tiles = ladder_rows(n_row, n_col, kt_local, shifts, ahead, mask, [held[s] for s in shifts], ints, out_shape, out)
    return pl.pallas_call(
        functools.partial(last_kernel, n_col, last),
        out_shape=out_shape,
        in_specs=[_vmem] * 3 + [_any],
        out_specs=_any,
        scratch_shapes=[pltpu.VMEM((rows, integrals.shape[1]), jnp.float32), pltpu.SemaphoreType.DMA],
        input_output_aliases={3: 0},
        compiler_params=_params,
    )(*held[last], *tiles, out)


def solution(mesh):
    placed = (P(("row", "col"), None), P("row", "col"), P("row", "col"), P("row", "col"))
    return jax.shard_map(
        functools.partial(on_device, mesh.shape["row"], mesh.shape["col"]),
        mesh=mesh,
        in_specs=placed,
        out_specs=P("row", "col"),
        check_vma=False,
    )
```
